1024 devices in a mesh: section: 32 (over y, z_hi, core), dp: 32 (over z_lo, x).
Axes of the slice: x: 4, y: 8, z: 16 (z_hi: 2, z_lo: 8; z = z_hi * 8 + z_lo), core: 2. Of those that a mesh axis runs over, the one named last changes fastest.
Arguments:
- latents: bfloat16 [6, 704, 1536], P(None, 'dp'), may hold values from -6 to 6
- control_hint: bfloat16 [6, 704, 1536], P(None, 'dp'), may hold values from -6 to 6
- upstream: bfloat16 [6, 704, 1536], P(None, 'dp'), may hold values from -6 to 6
- batch_order: int32 [6], replicated, may hold values from 0 to 5, each once
- section_weight: bfloat16 [32, 1536, 1536], P('section'), may hold values from -0.078125 to 0.078125
- zero_weight: bfloat16 [32, 768, 1536], P('section'), may hold values from -0.0390625 to 0.0390625
Outputs:
- zero_grad: float32 [32, 768, 1536], P('section', 'dp')
The draws below stay inside these ranges and needn't reach their ends.
Inputs may be any that keep to these rules, and one draw needn't show every extreme that they name: batch_order names each of the 6 micro-batches exactly once.
All inputs are finite; a program needn't handle non-finite values.
Results may differ from the reference program's by a relative error of at most 0.03.
Values may be sent and summed in bfloat16 or wider, within the bound.
No kernel may reach another device: no remote copies, remote signals or barrier semaphores. Data moves between devices by JAX's collectives and lax.ppermute only.
A program may use at most 32 MiB of HBM per device.

```python
import math
import jax
import jax.numpy as jnp
from jax import lax

D = 1536
MICRO = 6
ROWS = 22
TOKENS = 704
HALF = 768
N_SECTION = 32
N_DP = 32


def spiked(result, own_key, source, target, shards_of, factor):
    owner, partner = [(jnp.arange(result.shape[position]) // (result.shape[position] // shards_of)).reshape([-1 if axis == position else 1 for axis in range(result.ndim)]) for position in (source, target)]
    chosen = jax.random.permutation(own_key, shards_of)[partner]
    strong = (owner == chosen) | (owner == (partner + shards_of // 2) % shards_of)
    return jnp.where(strong, factor * result, result)


def steps_of(key, extent, cuts, smallest, top_value):
    level, own = 1.0, jax.random.fold_in(key, 6)
    for dim, blocks in cuts:
        steps = jnp.exp(jax.random.uniform(jax.random.fold_in(own, dim), (blocks,), jnp.float32, smallest / len(cuts), top_value / len(cuts)))
        level = level * jnp.repeat(steps, extent[dim] // blocks).reshape([-1 if axis == dim else 1 for axis in range(len(extent))])
    return level


def bell_draw(stream_key, dims, deviation, bound, shards=(), kind=jnp.bfloat16):
    values = jax.random.normal(stream_key, dims, jnp.float32) * deviation
    if len(shards) > 0:
        values = steps_of(stream_key, dims, shards, -0.22, 0.18) * values
    return jnp.clip(values, min=-bound, max=bound).astype(kind)


def gaussian_with(key, extent, scale, reach, shards, heavy, dtype=jnp.bfloat16):
    values = scale * jax.random.normal(key, extent, jnp.float32)
    if shards:
        values = values * steps_of(key, extent, shards, -0.22, 0.18)
    return jnp.clip(spiked(values, jax.random.fold_in(key, 3), *heavy), -reach, reach).astype(dtype)


def setup_inputs(seed: int = 0) -> dict:
    splits = jax.random.split(jax.random.key(seed), 7)
    return {
        "latents": bell_draw(splits[0], (MICRO, TOKENS, D), 1.0, 6.0, ((1, 32),)),
        "control_hint": gaussian_with(splits[1], (MICRO, TOKENS, D), 1.0, 6.0, ((1, 32),), (1, 2, 32, 2.75)),
        "upstream": bell_draw(splits[2], (MICRO, TOKENS, D), 1.0, 6.0, ((1, 32),)),
        "batch_order": jax.random.permutation(splits[3], MICRO).astype(jnp.int32),
        "section_weight": bell_draw(splits[4], (N_SECTION, D, D), (4 * D) ** -0.5, 0.078125, ((0, 32),)),
        "zero_weight": bell_draw(splits[5], (N_SECTION, HALF, D), (16 * D) ** -0.5, 0.0390625, ((0, 32),)),
    }


tanh_coef = 0.7978845608028654
cube_coef = 0.044715

def gelu_value(values):
    inner = tanh_coef * (values + cube_coef * values * values * values)
    return 0.5 * values * (1.0 + jnp.tanh(inner))

def gelu_slope(values):
    inner = tanh_coef * (values + cube_coef * values * values * values)
    tangent = jnp.tanh(inner)
    return 0.5 * (1.0 + tangent) + 0.5 * values * (1.0 - tangent * tangent) * tanh_coef * (1.0 + 3.0 * cube_coef * values * values)

def device_sums(left_rows, right_rows):
    left_split = left_rows.reshape(MICRO, N_DP, ROWS, -1).transpose(1, 0, 2, 3).reshape(N_DP, MICRO * ROWS, -1)
    right_split = right_rows.reshape(MICRO, N_DP, ROWS, -1).transpose(1, 0, 2, 3).reshape(N_DP, MICRO * ROWS, -1)
    pieces = jnp.einsum('prs,prd->psd', left_split.astype(jnp.float32), right_split.astype(jnp.float32))
    rounded = lax.optimization_barrier(pieces.astype(jnp.bfloat16)).astype(jnp.float32)
    return lax.optimization_barrier(jnp.sum(rounded, axis=0)) * (1.0 / math.sqrt(MICRO * TOKENS))

def reference(latents, control_hint, upstream, batch_order, section_weight, zero_weight):
    blocks = N_SECTION // 2
    half_width = D // 2
    ordered = jnp.take(latents, batch_order, axis=0).reshape(-1, D)
    hinted = jnp.take(control_hint, batch_order, axis=0).reshape(-1, D)
    current = (ordered.astype(jnp.float32) + hinted.astype(jnp.float32)).astype(jnp.bfloat16)
    states = []
    for block_index in range(blocks):
        product = jnp.dot(current, section_weight[2 * block_index + 1], preferred_element_type=jnp.float32)
        current = (current.astype(jnp.float32) + gelu_value(product)).astype(jnp.bfloat16)
        states.append(current)
    stream = ordered
    slopes = []
    for block_index in range(blocks):
        state_now = states[block_index]
        partial_residual = jnp.dot(state_now[:, half_width:], zero_weight[2 * block_index + 1], preferred_element_type=jnp.float32).astype(jnp.bfloat16)
        partial_back = lax.optimization_barrier(partial_residual).astype(jnp.float32)
        product = jnp.dot(stream, section_weight[2 * block_index], preferred_element_type=jnp.float32)
        residual_add = jnp.dot(state_now[:, :half_width], zero_weight[2 * block_index], preferred_element_type=jnp.float32) + partial_back
        slopes.append(gelu_slope(product))
        stream = (stream.astype(jnp.float32) + gelu_value(product) + residual_add).astype(jnp.bfloat16)
    grad_now = upstream.reshape(-1, D)
    pieces_all = [None] * (2 * blocks)
    for block_index in range(blocks - 1, -1, -1):
        state_now = states[block_index]
        pieces_all[2 * block_index] = device_sums(state_now[:, :half_width], grad_now)
        pieces_all[2 * block_index + 1] = device_sums(state_now[:, half_width:], grad_now)
        if block_index > 0:
            scaled = (grad_now.astype(jnp.float32) * slopes[block_index]).astype(jnp.bfloat16)
            back_term = jnp.dot(scaled, section_weight[2 * block_index].T, preferred_element_type=jnp.float32)
            grad_now = (grad_now.astype(jnp.float32) + back_term).astype(jnp.bfloat16)
    return jnp.stack(pieces_all)
```

```python
import functools
import math

import jax
import jax.numpy as jnp
from jax import lax
from jax.experimental import pallas as pl
from jax.experimental.pallas import tpu as pltpu
from jax.sharding import PartitionSpec as P

tanh_coef = 0.7978845608028654
cube_coef = 0.044715
chunk_count = 2
x_size = 4
both_axes = ("section", "dp")


def gelu_value(values):
    inner = tanh_coef * (values + cube_coef * values * values * values)
    return 0.5 * values * (1.0 + jnp.tanh(inner))


def gelu_slope(values):
    inner = tanh_coef * (values + cube_coef * values * values * values)
    tangent = jnp.tanh(inner)
    return 0.5 * (1.0 + tangent) + 0.5 * values * (1.0 - tangent * tangent) * tanh_coef * (
        1.0 + 3.0 * cube_coef * values * values
    )


in_vmem = pl.BlockSpec(memory_space=pltpu.VMEM)
in_smem = pl.BlockSpec(memory_space=pltpu.SMEM)


def local_call(kernel, operands, results, flops, aliases, scratch=()):
    return pl.pallas_call(
        kernel,
        out_shape=results,
        in_specs=[in_smem] + [in_vmem] * (len(operands) - 1),
        out_specs=tuple([in_vmem] * len(results)),
        input_output_aliases=aliases,
        scratch_shapes=scratch,
        compiler_params=pltpu.CompilerParams(vmem_limit_bytes=4 << 20),
        cost_estimate=pl.CostEstimate(flops=flops, bytes_accessed=flops // 256, transcendentals=0),
    )(*operands)


def shape_of(value, dtype=None):
    return jax.ShapeDtypeStruct(value.shape, dtype or value.dtype)


def columns_of(index, size):
    return pl.ds(pl.multiple_of(index * size, size), size)


def in_chunks(step):
    return (step >= 0) & (step < chunk_count)


def entry_rows(depth_now, first_depth, own, arrived, chosen):
    if arrived is None:
        return own
    if own is None:
        return arrived

    @pl.when(depth_now == first_depth)
    def _():
        chosen[...] = own[...]

    @pl.when(depth_now != first_depth)
    def _():
        chosen[...] = arrived[...]

    return chosen


def layer_kernel(step, has_arrived, has_own, *refs):
    refs = list(refs)
    place = refs.pop(0)
    arrived = refs.pop(0) if has_arrived else None
    own = refs.pop(0) if has_own else None
    residual, weight, kept_in, outgoing, kept, chosen = refs
    del kept_in
    is_base, depth = place[0], place[1]
    chunk = step - 1 - depth
    inputs = entry_rows(depth, 0, own, arrived, chosen)
    width = weight.shape[1]
    size = min(256, width)

    @pl.loop(0, width // size)
    def _(index):
        part = columns_of(index, size)
        product = jnp.dot(inputs[...], weight[:, part], preferred_element_type=jnp.float32)
        added = jnp.where(is_base == 1, residual[:, part], 0.0)
        total = inputs[:, part].astype(jnp.float32) + gelu_value(product) + added
        outgoing[:, part] = total.astype(jnp.bfloat16)

        @pl.when(in_chunks(chunk))
        def _():
            kept[jnp.clip(chunk, 0, chunk_count - 1), :, part] = product


def residual_kernel(
    step, place, received, outgoing, zero_rows, second_rows, sides_in, residual, sides
):
    del sides_in
    half, width = zero_rows.shape
    size = min(256, width)
    chunk = step - place[1]
    slot = jnp.clip(chunk, 0, chunk_count - 1)

    @pl.when(place[0] == 1)
    def _():
        @pl.loop(0, width // size)
        def _(index):
            part = columns_of(index, size)
            residual[:, part] = jnp.dot(
                received[:, :half], zero_rows[:, part], preferred_element_type=jnp.float32
            ) + jnp.dot(
                received[:, half:], second_rows[:, part], preferred_element_type=jnp.float32
            )

    @pl.when((place[0] == 1) & in_chunks(chunk))
    def _():
        sides[slot] = received[:, :half]

    @pl.when((place[0] == 0) & in_chunks(chunk))
    def _():
        sides[slot] = outgoing[:, half:]


def back_kernel(step, last_depth, has_arrived, has_own, has_slopes, *refs):
    refs = list(refs)
    place = refs.pop(0)
    arrived = refs.pop(0) if has_arrived else None
    own = refs.pop(0) if has_own else None
    if has_slopes:
        slopes, weight, kept_in, outgoing, kept, chosen, scaled = refs
    else:
        kept_in, kept, chosen = refs
    del kept_in
    chunk = step - (last_depth - place[1])
    slot = jnp.clip(chunk, 0, chunk_count - 1)
    grad = entry_rows(place[1], last_depth, own, arrived, chosen)

    if has_slopes:
        width = weight.shape[1]
        size = min(256, width)
        scaled[...] = (grad[...].astype(jnp.float32) * slopes[slot]).astype(jnp.bfloat16)

        @pl.loop(0, width // size)
        def _(index):
            part = columns_of(index, size)
            back_term = lax.dot_general(
                scaled[...],
                weight[part, :],
                (((1,), (1,)), ((), ())),
                preferred_element_type=jnp.float32,
            )
            outgoing[:, part] = (grad[:, part].astype(jnp.float32) + back_term).astype(
                jnp.bfloat16
            )

    @pl.when(in_chunks(chunk))
    def _():
        kept[slot] = grad[...]


def slope_kernel(products, slopes):
    width = products.shape[-1]
    size = min(256, width)

    @pl.loop(0, width // size)
    def _(index):
        part = columns_of(index, size)
        for chunk in range(chunk_count):
            slopes[chunk, :, part] = gelu_slope(products[chunk, :, part])


def body(latents, control_hint, upstream, batch_order, section_weight, zero_weight):
    section_count = lax.axis_size("section")
    dp_count = lax.axis_size("dp")
    z_size = dp_count // x_size
    block_count = section_count // 2
    section_place = lax.axis_index("section")
    dp_place = lax.axis_index("dp")
    x_place = dp_place % x_size
    z_place = dp_place // x_size
    depth = section_place // 2
    is_base = section_place % 2 == 0
    weight = section_weight[0]
    zero_rows = zero_weight[0]
    width = weight.shape[0]
    half = zero_rows.shape[0]
    all_rows = latents.shape[0] * latents.shape[1]
    rows = all_rows // chunk_count

    def mirrored(place):
        return (z_size - 1 - place // x_size) * x_size + place % x_size

    def move(value, section_pairs, flip):
        pairs = [
            (source * dp_count + place, target * dp_count + (mirrored(place) if flip else place))
            for source, target in section_pairs
            for place in range(dp_count)
        ]
        return lax.ppermute(value, both_axes, pairs)

    def active_blocks(step):
        return [
            step - chunk for chunk in range(chunk_count) if 0 <= step - chunk < block_count
        ]

    last_base = section_count - 2
    second_rows = move(
        zero_rows, [(2 * block + 1, 2 * block) for block in range(block_count)], False
    )
    upstream_rows = move(
        upstream.reshape(all_rows, width), [(last_base, last_base)], True
    ).reshape(chunk_count, rows, width)

    ordered = jnp.take(latents, batch_order, axis=0)
    hinted = jnp.take(control_hint, batch_order, axis=0)
    started = (ordered.astype(jnp.float32) + hinted.astype(jnp.float32)).astype(jnp.bfloat16)
    first_rows = jnp.where(is_base, ordered, started).reshape(chunk_count, rows, width)

    place = jnp.stack([is_base.astype(jnp.int32), depth])
    row_buffer = pltpu.VMEM((rows, width), jnp.bfloat16)
    row_shape = jax.ShapeDtypeStruct((rows, width), jnp.bfloat16)
    arrived = None
    residual = jnp.zeros((rows, width), jnp.float32)
    products = jnp.zeros((chunk_count, rows, width), jnp.float32)
    sides = jnp.zeros((chunk_count, rows, half), jnp.bfloat16)
    for step in range(block_count + chunk_count):
        entering = ()
        if arrived is not None:
            entering += (arrived,)
        if step <= chunk_count:
            entering += (
                jnp.where(
                    is_base, first_rows[max(step - 1, 0)], first_rows[min(step, chunk_count - 1)]
                ),
            )
        outgoing, products = local_call(
            functools.partial(layer_kernel, step, arrived is not None, step <= chunk_count),
            (place,) + entering + (residual, weight, products),
            (row_shape, shape_of(products)),
            2 * rows * width * width,
            {3 + len(entering): 1},
            (row_buffer,),
        )
        hops = [
            (2 * block + 1 - lag, 2 * block + 3 - lag)
            for lag in (0, 1)
            for block in active_blocks(step - lag)
            if block + 1 < block_count
        ]
        if hops:
            arrived = move(outgoing, hops, True)
        shares = [(2 * block + 1, 2 * block) for block in active_blocks(step)]
        if shares:
            received = move(outgoing, shares, False)
            residual, sides = local_call(
                functools.partial(residual_kernel, step),
                (place, received, outgoing, zero_rows, second_rows, sides),
                (shape_of(residual), shape_of(sides)),
                256,
                {5: 1},
            )

    (slopes,) = local_call(
        lambda unused, products_in, slopes_out: slope_kernel(products_in, slopes_out),
        (place, products),
        (shape_of(products),),
        256,
        {},
    )

    def along_x(value, shift, section_pairs=None):
        sections = range(section_count) if section_pairs is None else section_pairs
        pairs = [
            (section * dp_count + z * x_size + (x + shift) % x_size, section * dp_count + z * x_size + x)
            for section in sections
            for z in range(z_size)
            for x in range(x_size)
        ]
        return lax.ppermute(value, both_axes, pairs)

    base_sections = range(0, section_count, 2)

    def spread_side(side):
        source = lax.broadcasted_iota(jnp.int32, (half, half), 0)
        target = lax.broadcasted_iota(jnp.int32, (half, half), 1)
        quarter = half // x_size
        piece = quarter // z_size
        shift = target // quarter
        within = target % quarter
        wanted = (
            (within // piece) * piece * x_size
            + ((x_place - shift) % x_size) * piece
            + within % piece
        )
        picks = (source == wanted).astype(jnp.bfloat16)
        picked = jnp.dot(side, picks, preferred_element_type=jnp.float32).astype(jnp.bfloat16)
        parts = [picked[:, shift * quarter : (shift + 1) * quarter] for shift in range(x_size)]
        return [parts[0]] + [along_x(parts[shift], shift) for shift in range(1, x_size)]

    def spread_grad(grad):
        return jnp.concatenate(
            [grad] + [along_x(grad, shift, base_sections) for shift in range(1, x_size)], axis=0
        )

    def share_grad(gathered):
        shared = move(gathered, [(2 * block, 2 * block + 1) for block in range(block_count)], False)
        return jnp.where(is_base, gathered, shared)

    grads = jnp.zeros((chunk_count, rows, width), jnp.bfloat16)
    spread_sides = None
    grad_parts = [None] * chunk_count
    for step in range(block_count + chunk_count - 1):
        if step == block_count // 2:
            sides, arrived = lax.optimization_barrier((sides, arrived))
            spread = spread_side(sides.reshape(all_rows, half))
        if step == block_count // 2 + 2:
            spread, arrived = lax.optimization_barrier((spread, arrived))
            spread_sides = [
                jnp.concatenate([part[chunk * rows : (chunk + 1) * rows] for part in spread])
                for chunk in range(chunk_count)
            ]
        entering = ()
        if step > 0:
            entering += (arrived,)
        if step < chunk_count:
            entering += (upstream_rows[step],)
        hops = [
            (2 * (block_count - 1 - back), 2 * (block_count - 2 - back))
            for back in active_blocks(step)
            if back + 1 < block_count
        ]
        done_chunk = step - (block_count - 1)
        grad_in = arrived
        if hops:
            outgoing, grads = local_call(
                functools.partial(
                    back_kernel, step, block_count - 1, step > 0, step < chunk_count, True
                ),
                (place,) + entering + (slopes, weight, grads),
                (row_shape, shape_of(grads)),
                2 * rows * width * width,
                {3 + len(entering): 1},
                (row_buffer, row_buffer),
            )
            arrived = move(outgoing, hops, True)
        if 0 <= done_chunk < chunk_count - 1:
            gathered = spread_grad(grads[done_chunk])
            gathered, arrived = lax.optimization_barrier((gathered, arrived))
        elif done_chunk >= 0:
            gathered = spread_grad(jnp.where(depth == 0, grad_in, grads[done_chunk]))
        if done_chunk >= 0:
            grad_parts[done_chunk] = lax.dot_general(
                spread_sides[done_chunk],
                share_grad(gathered),
                (((0,), (0,)), ((), ())),
                preferred_element_type=jnp.float32,
            )

    partial_value = sum(grad_parts[1:], grad_parts[0]).reshape(
        z_size, half // dp_count, width
    )
    distance = z_size // 2
    while distance:
        upper = (z_place // distance) % 2
        kept = lax.dynamic_slice_in_dim(partial_value, upper * distance, distance, 0)
        sent = lax.dynamic_slice_in_dim(partial_value, (1 - upper) * distance, distance, 0)
        pairs = [
            (place, ((place // x_size) ^ distance) * x_size + place % x_size)
            for place in range(dp_count)
        ]
        partial_value = kept + lax.ppermute(sent.astype(jnp.bfloat16), "dp", pairs).astype(
            jnp.float32
        )
        distance //= 2
    grad_scale = 1.0 / math.sqrt(all_rows * dp_count)
    return partial_value * grad_scale


def solution(mesh):
    placed = (
        P(None, "dp", None),
        P(None, "dp", None),
        P(None, "dp", None),
        P(),
        P("section", None, None),
        P("section", None, None),
    )
    return jax.shard_map(
        body, mesh=mesh, in_specs=placed, out_specs=P("section", "dp", None), check_vma=False
    )
```

```python
import functools
import math

import jax
import jax.numpy as jnp
from jax import lax
from jax.experimental import pallas as pl
from jax.experimental.pallas import tpu as pltpu
from jax.sharding import PartitionSpec as P

tanh_coef = 0.7978845608028654
cube_coef = 0.044715
chunk_count = 2
x_size = 4
both_axes = ("section", "dp")


def gelu_value(values):
    inner = tanh_coef * (values + cube_coef * values * values * values)
    return 0.5 * values * (1.0 + jnp.tanh(inner))


def gelu_slope(values):
    inner = tanh_coef * (values + cube_coef * values * values * values)
    tangent = jnp.tanh(inner)
    return 0.5 * (1.0 + tangent) + 0.5 * values * (1.0 - tangent * tangent) * tanh_coef * (
        1.0 + 3.0 * cube_coef * values * values
    )


in_vmem = pl.BlockSpec(memory_space=pltpu.VMEM)
in_smem = pl.BlockSpec(memory_space=pltpu.SMEM)


def local_call(kernel, operands, results, flops, aliases, scratch=()):
    return pl.pallas_call(
        kernel,
        out_shape=results,
        in_specs=[in_smem] + [in_vmem] * (len(operands) - 1),
        out_specs=tuple([in_vmem] * len(results)),
        input_output_aliases=aliases,
        scratch_shapes=scratch,
        compiler_params=pltpu.CompilerParams(vmem_limit_bytes=4 << 20),
        cost_estimate=pl.CostEstimate(flops=flops, bytes_accessed=flops // 256, transcendentals=0),
    )(*operands)


def shape_of(value, dtype=None):
    return jax.ShapeDtypeStruct(value.shape, dtype or value.dtype)


def columns_of(index, size):
    return pl.ds(pl.multiple_of(index * size, size), size)


def in_chunks(step):
    return (step >= 0) & (step < chunk_count)


def entry_rows(depth_now, first_depth, own, arrived, chosen):
    if arrived is None:
        return own
    if own is None:
        return arrived

    @pl.when(depth_now == first_depth)
    def _():
        chosen[...] = own[...]

    @pl.when(depth_now != first_depth)
    def _():
        chosen[...] = arrived[...]

    return chosen


def layer_kernel(step, has_arrived, has_own, *refs):
    refs = list(refs)
    place = refs.pop(0)
    arrived = refs.pop(0) if has_arrived else None
    own = refs.pop(0) if has_own else None
    residual, weight, kept_in, outgoing, kept, chosen = refs
    del kept_in
    is_base, depth = place[0], place[1]
    chunk = step - 1 - depth
    inputs = entry_rows(depth, 0, own, arrived, chosen)
    width = weight.shape[1]
    size = min(256, width)

    @pl.loop(0, width // size)
    def _(index):
        part = columns_of(index, size)
        product = jnp.dot(inputs[...], weight[:, part], preferred_element_type=jnp.float32)
        added = jnp.where(is_base == 1, residual[:, part], 0.0)
        total = inputs[:, part].astype(jnp.float32) + gelu_value(product) + added
        outgoing[:, part] = total.astype(jnp.bfloat16)

        @pl.when(in_chunks(chunk))
        def _():
            kept[jnp.clip(chunk, 0, chunk_count - 1), :, part] = product


def residual_kernel(step, place, received, zero_rows, second_rows, sides_in, residual, sides):
    del sides_in
    half, width = zero_rows.shape
    size = min(256, width)
    chunk = step - place[1]
    slot = jnp.clip(chunk, 0, chunk_count - 1)

    @pl.when(place[0] == 1)
    def _():
        @pl.loop(0, width // size)
        def _(index):
            part = columns_of(index, size)
            residual[:, part] = jnp.dot(
                received[:, :half], zero_rows[:, part], preferred_element_type=jnp.float32
            ) + jnp.dot(
                received[:, half:], second_rows[:, part], preferred_element_type=jnp.float32
            )

    @pl.when((place[0] == 1) & in_chunks(chunk))
    def _():
        sides[slot] = received[...]


def back_kernel(step, last_depth, has_arrived, has_own, has_slopes, *refs):
    refs = list(refs)
    place = refs.pop(0)
    arrived = refs.pop(0) if has_arrived else None
    own = refs.pop(0) if has_own else None
    if has_slopes:
        slopes, weight, kept_in, outgoing, kept, chosen, scaled = refs
    else:
        kept_in, kept, chosen = refs
    del kept_in
    chunk = step - (last_depth - place[1])
    slot = jnp.clip(chunk, 0, chunk_count - 1)
    grad = entry_rows(place[1], last_depth, own, arrived, chosen)

    if has_slopes:
        width = weight.shape[1]
        size = min(256, width)
        scaled[...] = (grad[...].astype(jnp.float32) * slopes[slot]).astype(jnp.bfloat16)

        @pl.loop(0, width // size)
        def _(index):
            part = columns_of(index, size)
            back_term = lax.dot_general(
                scaled[...],
                weight[part, :],
                (((1,), (1,)), ((), ())),
                preferred_element_type=jnp.float32,
            )
            outgoing[:, part] = (grad[:, part].astype(jnp.float32) + back_term).astype(
                jnp.bfloat16
            )

    @pl.when(in_chunks(chunk))
    def _():
        kept[slot] = grad[...]


def slope_kernel(products, slopes):
    width = products.shape[-1]
    size = min(256, width)

    @pl.loop(0, width // size)
    def _(index):
        part = columns_of(index, size)
        for chunk in range(chunk_count):
            slopes[chunk, :, part] = gelu_slope(products[chunk, :, part])


def body(latents, control_hint, upstream, batch_order, section_weight, zero_weight):
    section_count = lax.axis_size("section")
    dp_count = lax.axis_size("dp")
    z_size = dp_count // x_size
    block_count = section_count // 2
    section_place = lax.axis_index("section")
    dp_place = lax.axis_index("dp")
    x_place = dp_place % x_size
    z_place = dp_place // x_size
    depth = section_place // 2
    is_base = section_place % 2 == 0
    weight = section_weight[0]
    zero_rows = zero_weight[0]
    width = weight.shape[0]
    half = zero_rows.shape[0]
    all_rows = latents.shape[0] * latents.shape[1]
    rows = all_rows // chunk_count

    def mirrored(place):
        return (z_size - 1 - place // x_size) * x_size + place % x_size

    def move(value, section_pairs, flip):
        pairs = [
            (source * dp_count + place, target * dp_count + (mirrored(place) if flip else place))
            for source, target in section_pairs
            for place in range(dp_count)
        ]
        return lax.ppermute(value, both_axes, pairs)

    def active_blocks(step):
        return [
            step - chunk for chunk in range(chunk_count) if 0 <= step - chunk < block_count
        ]

    to_base = [(2 * block + 1, 2 * block) for block in range(block_count)]
    to_control = [(2 * block, 2 * block + 1) for block in range(block_count)]

    def forward_hops(step):
        last = block_count + chunk_count - 2
        if step < 3:
            steps = range(3)
        elif step > last - 3:
            steps = range(last - 2, last + 1)
        else:
            steps = (step,)
        return sorted(
            {
                (2 * block + 1 - lag, 2 * block + 3 - lag)
                for each in steps
                for lag in (0, 1)
                for block in active_blocks(each - lag)
                if block + 1 < block_count
            }
        )

    def backward_hops(step):
        last = block_count + chunk_count - 3
        if step < 3:
            steps = range(3)
        elif step > last - 2:
            steps = range(last - 1, last + 1)
        else:
            steps = (step,)
        return sorted(
            {
                (2 * (block_count - 1 - back), 2 * (block_count - 2 - back))
                for each in steps
                for back in active_blocks(each)
                if back + 1 < block_count
            }
        )

    second_rows = move(zero_rows, to_base, False)
    upstream_rows = move(
        upstream.reshape(all_rows, width), forward_hops(block_count), True
    ).reshape(chunk_count, rows, width)

    ordered = jnp.take(latents, batch_order, axis=0)
    hinted = jnp.take(control_hint, batch_order, axis=0)
    started = (ordered.astype(jnp.float32) + hinted.astype(jnp.float32)).astype(jnp.bfloat16)
    first_rows = jnp.where(is_base, ordered, started).reshape(chunk_count, rows, width)

    place = jnp.stack([is_base.astype(jnp.int32), depth])
    row_buffer = pltpu.VMEM((rows, width), jnp.bfloat16)
    row_shape = jax.ShapeDtypeStruct((rows, width), jnp.bfloat16)
    arrived = None
    residual = jnp.zeros((rows, width), jnp.float32)
    products = jnp.zeros((chunk_count, rows, width), jnp.float32)
    sides = jnp.zeros((chunk_count, rows, width), jnp.bfloat16)
    for step in range(block_count + chunk_count):
        entering = ()
        if arrived is not None:
            entering += (arrived,)
        if step <= chunk_count:
            entering += (
                jnp.where(
                    is_base, first_rows[max(step - 1, 0)], first_rows[min(step, chunk_count - 1)]
                ),
            )
        outgoing, products = local_call(
            functools.partial(layer_kernel, step, arrived is not None, step <= chunk_count),
            (place,) + entering + (residual, weight, products),
            (row_shape, shape_of(products)),
            2 * rows * width * width,
            {3 + len(entering): 1},
            (row_buffer,),
        )
        if step < block_count + chunk_count - 1:
            arrived = move(outgoing, forward_hops(step), True)
        if step < block_count + chunk_count - 1:
            received = move(outgoing, to_base, False)
            residual, sides = local_call(
                functools.partial(residual_kernel, step),
                (place, received, zero_rows, second_rows, sides),
                (shape_of(residual), shape_of(sides)),
                256,
                {4: 1},
            )

    (slopes,) = local_call(
        lambda unused, products_in, slopes_out: slope_kernel(products_in, slopes_out),
        (place, products),
        (shape_of(products),),
        256,
        {},
    )

    def along_x(value, shift):
        pairs = [
            (section * dp_count + z * x_size + (x + shift) % x_size, section * dp_count + z * x_size + x)
            for section in range(0, section_count, 2)
            for z in range(z_size)
            for x in range(x_size)
        ]
        return lax.ppermute(value, both_axes, pairs)

    quarter = half // x_size

    def spread_side(side):
        source = lax.broadcasted_iota(jnp.int32, (half, half), 0)
        target = lax.broadcasted_iota(jnp.int32, (half, half), 1)
        piece = quarter // z_size
        shift = target // quarter
        within = target % quarter
        wanted = (
            (within // piece) * piece * x_size
            + ((x_place - shift) % x_size) * piece
            + within % piece
        )
        picks = (source == wanted).astype(jnp.bfloat16)
        picked = [
            jnp.dot(part, picks, preferred_element_type=jnp.float32).astype(jnp.bfloat16)
            for part in (side[:, :half], side[:, half:])
        ]
        parts = [
            jnp.concatenate(
                [part[:, shift * quarter : (shift + 1) * quarter] for part in picked], axis=1
            )
            for shift in range(x_size)
        ]
        return [parts[0]] + [along_x(parts[shift], shift) for shift in range(1, x_size)]

    def spread_grad(grad):
        return jnp.concatenate(
            [grad] + [along_x(grad, shift) for shift in range(1, x_size)], axis=0
        )

    grads = jnp.zeros((chunk_count, rows, width), jnp.bfloat16)
    spread_sides = None
    grad_parts = [None] * chunk_count
    for step in range(block_count + chunk_count - 1):
        if step == block_count // 2:
            sides, arrived = lax.optimization_barrier((sides, arrived))
            spread = spread_side(sides.reshape(all_rows, width))
        if step == block_count // 2 + 2:
            spread_sides = [
                jnp.concatenate([part[chunk * rows : (chunk + 1) * rows] for part in spread])
                for chunk in range(chunk_count)
            ]
            spread_sides, arrived = lax.optimization_barrier((spread_sides, arrived))
        entering = ()
        if step > 0:
            entering += (arrived,)
        if step < chunk_count:
            entering += (upstream_rows[step],)
        done_chunk = step - (block_count - 1)
        grad_in = arrived
        if step < block_count + chunk_count - 2:
            outgoing, grads = local_call(
                functools.partial(
                    back_kernel, step, block_count - 1, step > 0, step < chunk_count, True
                ),
                (place,) + entering + (slopes, weight, grads),
                (row_shape, shape_of(grads)),
                2 * rows * width * width,
                {3 + len(entering): 1},
                (row_buffer, row_buffer),
            )
            arrived = move(outgoing, backward_hops(step), True)
        if 0 <= done_chunk < chunk_count - 1:
            gathered = spread_grad(grads[done_chunk])
            gathered, arrived = lax.optimization_barrier((gathered, arrived))
        elif done_chunk >= 0:
            gathered = spread_grad(jnp.where(depth == 0, grad_in, grads[done_chunk]))
        if done_chunk >= 0:
            grad_parts[done_chunk] = lax.dot_general(
                spread_sides[done_chunk],
                gathered,
                (((0,), (0,)), ((), ())),
                preferred_element_type=jnp.float32,
            )

    both_values = sum(grad_parts[1:], grad_parts[0])
    control_value = move(both_values[quarter:].astype(jnp.bfloat16), to_control, False)
    partial_value = jnp.where(
        is_base, both_values[:quarter], control_value.astype(jnp.float32)
    ).reshape(z_size, half // dp_count, width)
    distance = z_size // 2
    while distance:
        upper = (z_place // distance) % 2
        kept = lax.dynamic_slice_in_dim(partial_value, upper * distance, distance, 0)
        sent = lax.dynamic_slice_in_dim(partial_value, (1 - upper) * distance, distance, 0)
        pairs = [
            (place, ((place // x_size) ^ distance) * x_size + place % x_size)
            for place in range(dp_count)
        ]
        partial_value = kept + lax.ppermute(sent.astype(jnp.bfloat16), "dp", pairs).astype(
            jnp.float32
        )
        distance //= 2
    grad_scale = 1.0 / math.sqrt(all_rows * dp_count)
    return partial_value * grad_scale


def solution(mesh):
    placed = (
        P(None, "dp", None),
        P(None, "dp", None),
        P(None, "dp", None),
        P(),
        P("section", None, None),
        P("section", None, None),
    )
    return jax.shard_map(
        body, mesh=mesh, in_specs=placed, out_specs=P("section", "dp", None), check_vma=False
    )
```

```python
import functools
import math

import jax
import jax.numpy as jnp
from jax import lax
from jax.experimental import pallas as pl
from jax.experimental.pallas import tpu as pltpu
from jax.sharding import PartitionSpec as P

tanh_coef = 0.7978845608028654
cube_coef = 0.044715
chunk_count = 2
x_size = 4
both_axes = ("section", "dp")
tile = 768


def gelu_value(values):
    inner = tanh_coef * (values + cube_coef * values * values * values)
    return 0.5 * values * (1.0 + jnp.tanh(inner))


def gelu_slope(values):
    inner = tanh_coef * (values + cube_coef * values * values * values)
    tangent = jnp.tanh(inner)
    return 0.5 * (1.0 + tangent) + 0.5 * values * (1.0 - tangent * tangent) * tanh_coef * (
        1.0 + 3.0 * cube_coef * values * values
    )


in_vmem = pl.BlockSpec(memory_space=pltpu.VMEM)
in_smem = pl.BlockSpec(memory_space=pltpu.SMEM)


def local_call(kernel, operands, results, flops, aliases, scratch=()):
    return pl.pallas_call(
        kernel,
        out_shape=results,
        in_specs=[in_smem] + [in_vmem] * (len(operands) - 1),
        out_specs=tuple([in_vmem] * len(results)),
        input_output_aliases=aliases,
        scratch_shapes=scratch,
        compiler_params=pltpu.CompilerParams(vmem_limit_bytes=4 << 20),
        cost_estimate=pl.CostEstimate(flops=flops, bytes_accessed=flops // 256, transcendentals=0),
    )(*operands)


def shape_of(value, dtype=None):
    return jax.ShapeDtypeStruct(value.shape, dtype or value.dtype)


def columns_of(index, size):
    return pl.ds(pl.multiple_of(index * size, size), size)


def in_chunks(step):
    return (step >= 0) & (step < chunk_count)


def entry_rows(depth_now, first_depth, own, arrived, chosen):
    if arrived is None:
        return own
    if own is None:
        return arrived

    @pl.when(depth_now == first_depth)
    def _():
        chosen[...] = own[...]

    @pl.when(depth_now != first_depth)
    def _():
        chosen[...] = arrived[...]

    return chosen


def layer_kernel(step, has_arrived, has_own, *refs):
    refs = list(refs)
    place = refs.pop(0)
    arrived = refs.pop(0) if has_arrived else None
    own = refs.pop(0) if has_own else None
    residual, weight, kept_in, outgoing, kept, chosen = refs
    del kept_in
    is_base, depth = place[0], place[1]
    chunk = step - 1 - depth
    inputs = entry_rows(depth, 0, own, arrived, chosen)
    width = weight.shape[1]
    size = min(tile, width)

    @pl.loop(0, width // size)
    def _(index):
        part = columns_of(index, size)
        product = jnp.dot(inputs[...], weight[:, part], preferred_element_type=jnp.float32)
        added = jnp.where(is_base == 1, residual[:, part], 0.0)
        total = inputs[:, part].astype(jnp.float32) + gelu_value(product) + added
        outgoing[:, part] = total.astype(jnp.bfloat16)

        @pl.when(in_chunks(chunk))
        def _():
            kept[jnp.clip(chunk, 0, chunk_count - 1), :, part] = product


def residual_kernel(
    step, place, received, outgoing, zero_rows, second_rows, sides_in, residual, sides
):
    del sides_in
    half, width = zero_rows.shape
    size = min(tile // 3, width)
    chunk = step - place[1]
    slot = jnp.clip(chunk, 0, chunk_count - 1)

    @pl.when(place[0] == 1)
    def _():
        @pl.loop(0, width // size)
        def _(index):
            part = columns_of(index, size)
            residual[:, part] = jnp.dot(
                received[:, :half], zero_rows[:, part], preferred_element_type=jnp.float32
            ) + jnp.dot(
                received[:, half:], second_rows[:, part], preferred_element_type=jnp.float32
            )

    @pl.when((place[0] == 0) & in_chunks(chunk))
    def _():
        sides[slot] = outgoing[...]


def back_kernel(step, last_depth, has_arrived, has_own, *refs):
    refs = list(refs)
    place = refs.pop(0)
    arrived = refs.pop(0) if has_arrived else None
    own = refs.pop(0) if has_own else None
    slopes, weight, kept_in, outgoing, kept, chosen, scaled = refs
    del kept_in
    chunk = step - (last_depth - place[1])
    slot = jnp.clip(chunk, 0, chunk_count - 1)
    grad = entry_rows(place[1], last_depth, own, arrived, chosen)
    width = weight.shape[1]
    size = min(tile, width)
    scaled[...] = (grad[...].astype(jnp.float32) * slopes[slot]).astype(jnp.bfloat16)

    @pl.loop(0, width // size)
    def _(index):
        part = columns_of(index, size)
        back_term = lax.dot_general(
            scaled[...],
            weight[part, :],
            (((1,), (1,)), ((), ())),
            preferred_element_type=jnp.float32,
        )
        outgoing[:, part] = (grad[:, part].astype(jnp.float32) + back_term).astype(jnp.bfloat16)

    @pl.when(in_chunks(chunk))
    def _():
        kept[slot] = grad[...]


def spread_kernel(place, sides, picks, *parts):
    half = picks.shape[1]

    @pl.when(place[0] == 0)
    def _():
        for shift, part in enumerate(parts):
            for chunk in range(chunk_count):
                for second in range(2):
                    part[chunk, second] = jnp.dot(
                        sides[chunk, :, second * half : (second + 1) * half],
                        picks[shift],
                        preferred_element_type=jnp.float32,
                    ).astype(jnp.bfloat16)


def finish_kernel(place, arrived, shared, kept, grads):
    @pl.when(place[1] == 0)
    def _():
        for chunk in range(chunk_count - 1):
            grads[chunk] = kept[chunk]
        grads[chunk_count - 1] = arrived[...]

    @pl.when(place[1] != 0)
    def _():
        grads[...] = shared[...]


def reduce_kernel(place, *refs):
    parts, grads, (second_value, first_value) = refs[:x_size], refs[x_size : 2 * x_size], refs[-2:]
    width = first_value.shape[1]
    size = min(512, width)

    @pl.when(place[0] == 0)
    def _():
        @pl.loop(0, width // size)
        def _(index):
            columns = columns_of(index, size)
            for second, target in enumerate((first_value, second_value)):
                total = None
                for part, grad in zip(parts, grads):
                    for chunk in range(chunk_count):
                        term = lax.dot_general(
                            part[chunk, second],
                            grad[chunk, :, columns],
                            (((0,), (0,)), ((), ())),
                            preferred_element_type=jnp.float32,
                        )
                        total = term if total is None else total + term
                target[:, columns] = total.astype(target.dtype)


def slope_kernel(products, slopes):
    width = products.shape[-1]
    size = min(256, width)

    @pl.loop(0, width // size)
    def _(index):
        part = columns_of(index, size)
        for chunk in range(chunk_count):
            slopes[chunk, :, part] = gelu_slope(products[chunk, :, part])


def body(latents, control_hint, upstream, batch_order, section_weight, zero_weight):
    section_count = lax.axis_size("section")
    dp_count = lax.axis_size("dp")
    z_size = dp_count // x_size
    block_count = section_count // 2
    section_place = lax.axis_index("section")
    dp_place = lax.axis_index("dp")
    x_place = dp_place % x_size
    z_place = dp_place // x_size
    depth = section_place // 2
    is_base = section_place % 2 == 0
    weight = section_weight[0]
    zero_rows = zero_weight[0]
    width = weight.shape[0]
    half = zero_rows.shape[0]
    all_rows = latents.shape[0] * latents.shape[1]
    rows = all_rows // chunk_count

    def mirrored(place):
        return (z_size - 1 - place // x_size) * x_size + place % x_size

    def move(value, section_pairs, flip):
        pairs = [
            (source * dp_count + place, target * dp_count + (mirrored(place) if flip else place))
            for source, target in section_pairs
            for place in range(dp_count)
        ]
        return lax.ppermute(value, both_axes, pairs)

    def active_blocks(step):
        return [
            step - chunk for chunk in range(chunk_count) if 0 <= step - chunk < block_count
        ]

    to_base = [(2 * block + 1, 2 * block) for block in range(block_count)]
    to_control = [(2 * block, 2 * block + 1) for block in range(block_count)]

    def forward_hops(step):
        last = block_count + chunk_count - 2
        if step < 3:
            steps = range(3)
        elif step > last - 3:
            steps = range(last - 2, last + 1)
        else:
            steps = (step,)
        return sorted(
            {
                (2 * block + 1 - lag, 2 * block + 3 - lag)
                for each in steps
                for lag in (0, 1)
                for block in active_blocks(each - lag)
                if block + 1 < block_count
            }
        )

    def backward_hops(step):
        last = block_count + chunk_count - 3
        if step < 3:
            steps = range(3)
        elif step > last - 2:
            steps = range(last - 1, last + 1)
        else:
            steps = (step,)
        return sorted(
            {
                (
                    2 * (block_count - 1 - back),
                    max(1, 2 * (block_count - 2 - back)),
                )
                for each in steps
                for back in active_blocks(each)
                if back + 1 < block_count
            }
        )

    second_rows = move(zero_rows, to_base, False)
    ordered = jnp.take(latents, batch_order, axis=0)
    hinted = jnp.take(control_hint, batch_order, axis=0)
    started = (ordered.astype(jnp.float32) + hinted.astype(jnp.float32)).astype(jnp.bfloat16)
    first_rows = jnp.where(is_base, ordered, started).reshape(chunk_count, rows, width)
    own_upstream = upstream.reshape(chunk_count, rows, width)
    first_rows = [first_rows[chunk] for chunk in range(chunk_count)]
    own_upstream = [own_upstream[chunk] for chunk in range(chunk_count)]
    quarter = half // x_size
    pick_shape = (x_size, half, quarter)
    piece = quarter // z_size
    within = lax.broadcasted_iota(jnp.int32, pick_shape, 2)
    order = within // piece
    z_target = jnp.zeros_like(order)
    distance = 1
    while distance < z_size:
        z_target = z_target + (order // (z_size // (2 * distance))) % 2 * distance
        distance *= 2
    x_target = (x_place - lax.broadcasted_iota(jnp.int32, pick_shape, 0)) % x_size
    wanted = (z_target * x_size + x_target) * piece + within % piece
    picks = (lax.broadcasted_iota(jnp.int32, pick_shape, 1) == wanted).astype(jnp.bfloat16)
    first_rows, own_upstream, picks = lax.optimization_barrier((first_rows, own_upstream, picks))
    upstream_rows = [move(part, forward_hops(block_count), True) for part in own_upstream]

    place = jnp.stack([is_base.astype(jnp.int32), depth])
    row_buffer = pltpu.VMEM((rows, width), jnp.bfloat16)
    row_shape = jax.ShapeDtypeStruct((rows, width), jnp.bfloat16)
    arrived = None
    residual = jnp.zeros((rows, width), jnp.float32)
    products = jnp.zeros((chunk_count, rows, width), jnp.float32)
    sides = jnp.zeros((chunk_count, rows, width), jnp.bfloat16)
    for step in range(block_count + chunk_count):
        entering = ()
        if step == 4:
            upstream_rows, arrived = lax.optimization_barrier((upstream_rows, arrived))
        if arrived is not None:
            entering += (arrived,)
        if step <= chunk_count:
            entering += (
                jnp.where(
                    is_base, first_rows[max(step - 1, 0)], first_rows[min(step, chunk_count - 1)]
                ),
            )
        outgoing, products = local_call(
            functools.partial(layer_kernel, step, arrived is not None, step <= chunk_count),
            (place,) + entering + (residual, weight, products),
            (row_shape, shape_of(products)),
            2 * rows * width * width,
            {3 + len(entering): 1},
            (row_buffer,),
        )
        if step < block_count + chunk_count - 1:
            arrived = move(outgoing, forward_hops(step), True)
        if step < block_count + chunk_count - 1:
            received = move(outgoing, to_base, False)
            residual, sides = local_call(
                functools.partial(residual_kernel, step),
                (place, received, outgoing, zero_rows, second_rows, sides),
                (shape_of(residual), shape_of(sides)),
                256,
                {5: 1},
            )

    (slopes,) = local_call(
        lambda unused, products_in, slopes_out: slope_kernel(products_in, slopes_out),
        (place, products),
        (shape_of(products),),
        256,
        {},
    )

    def along_x(value, shift):
        pairs = [
            (section * dp_count + z * x_size + (x + shift) % x_size, section * dp_count + z * x_size + x)
            for section in range(1, section_count, 2)
            for z in range(z_size)
            for x in range(x_size)
        ]
        return lax.ppermute(value, both_axes, pairs)

    def spread_side(side):
        part_shape = jax.ShapeDtypeStruct((chunk_count, 2, rows, quarter), jnp.bfloat16)
        parts = local_call(spread_kernel, (place, side, picks), (part_shape,) * x_size, 256, {})
        return [parts[0]] + [along_x(parts[shift], shift) for shift in range(1, x_size)]

    grads = jnp.zeros((chunk_count, rows, width), jnp.bfloat16)
    spread = joined = None
    for step in range(block_count + chunk_count - 1):
        if step == block_count // 2:
            joined = sides
        if step == block_count // 2 + 1:
            spread, arrived = lax.optimization_barrier((spread, arrived))
        entering = ()
        if step > 0:
            entering += (arrived,)
        if step < chunk_count:
            entering += (upstream_rows[step],)
        if step < block_count + chunk_count - 2:
            outgoing, grads = local_call(
                functools.partial(
                    back_kernel, step, block_count - 1, step > 0, step < chunk_count
                ),
                (place,) + entering + (slopes, weight, grads),
                (row_shape, shape_of(grads)),
                2 * rows * width * width,
                {3 + len(entering): 1},
                (row_buffer, row_buffer),
            )
            arrived = move(outgoing, backward_hops(step), True)
            if step == block_count // 2:
                joined, outgoing = lax.optimization_barrier((joined, outgoing))
                spread = spread_side(joined)

    (grads,) = local_call(
        finish_kernel,
        (place, arrived, move(grads, to_control, False), grads),
        (shape_of(grads),),
        256,
        {},
    )
    value_shape = (quarter, width)
    control_value, base_value = local_call(
        reduce_kernel,
        (place, *spread, grads) + tuple(along_x(grads, shift) for shift in range(1, x_size)),
        (
            jax.ShapeDtypeStruct(value_shape, jnp.float32),
            jax.ShapeDtypeStruct(value_shape, jnp.bfloat16),
        ),
        256,
        {},
    )
    base_value = move(base_value, to_base, False)
    partial_value = jnp.where(is_base, base_value.astype(jnp.float32), control_value).reshape(
        z_size, half // dp_count, width
    )
    distance = 1
    while distance < z_size:
        upper = (z_place // distance) % 2
        kept_size = partial_value.shape[0] // 2
        kept = lax.dynamic_slice_in_dim(partial_value, upper * kept_size, kept_size, 0)
        sent = lax.dynamic_slice_in_dim(partial_value, (1 - upper) * kept_size, kept_size, 0)
        pairs = [
            (place, ((place // x_size) ^ distance) * x_size + place % x_size)
            for place in range(dp_count)
        ]
        partial_value = kept + lax.ppermute(sent.astype(jnp.bfloat16), "dp", pairs).astype(
            jnp.float32
        )
        distance *= 2
    grad_scale = 1.0 / math.sqrt(all_rows * dp_count)
    return partial_value * grad_scale


def solution(mesh):
    placed = (
        P(None, "dp", None),
        P(None, "dp", None),
        P(None, "dp", None),
        P(),
        P("section", None, None),
        P("section", None, None),
    )
    return jax.shard_map(
        body, mesh=mesh, in_specs=placed, out_specs=P("section", "dp", None), check_vma=False
    )
```

```python
import functools
import math

import jax
import jax.numpy as jnp
from jax import lax
from jax.experimental import pallas as pl
from jax.experimental.pallas import tpu as pltpu
from jax.sharding import PartitionSpec as P

tanh_coef = 0.7978845608028654
cube_coef = 0.044715
chunk_count = 2
x_size = 4
both_axes = ("section", "dp")
tile = 768


def gelu_value(values):
    inner = tanh_coef * (values + cube_coef * values * values * values)
    return 0.5 * values * (1.0 + jnp.tanh(inner))


def gelu_slope(values):
    inner = tanh_coef * (values + cube_coef * values * values * values)
    tangent = jnp.tanh(inner)
    return 0.5 * (1.0 + tangent) + 0.5 * values * (1.0 - tangent * tangent) * tanh_coef * (
        1.0 + 3.0 * cube_coef * values * values
    )


in_vmem = pl.BlockSpec(memory_space=pltpu.VMEM)
in_smem = pl.BlockSpec(memory_space=pltpu.SMEM)


def local_call(kernel, operands, results, flops, aliases, scratch=()):
    return pl.pallas_call(
        kernel,
        out_shape=results,
        in_specs=[in_smem] + [in_vmem] * (len(operands) - 1),
        out_specs=tuple([in_vmem] * len(results)),
        input_output_aliases=aliases,
        scratch_shapes=scratch,
        compiler_params=pltpu.CompilerParams(vmem_limit_bytes=4 << 20),
        cost_estimate=pl.CostEstimate(flops=flops, bytes_accessed=flops // 256, transcendentals=0),
    )(*operands)


def shape_of(value, dtype=None):
    return jax.ShapeDtypeStruct(value.shape, dtype or value.dtype)


def columns_of(index, size):
    return pl.ds(pl.multiple_of(index * size, size), size)


def in_chunks(step):
    return (step >= 0) & (step < chunk_count)


def entry_rows(depth_now, first_depth, own, arrived, chosen):
    if arrived is None:
        return own
    if own is None:
        return arrived

    @pl.when(depth_now == first_depth)
    def _():
        chosen[...] = own[...]

    @pl.when(depth_now != first_depth)
    def _():
        chosen[...] = arrived[...]

    return chosen


def layer_kernel(step, has_arrived, has_own, *refs):
    refs = list(refs)
    place = refs.pop(0)
    arrived = refs.pop(0) if has_arrived else None
    own = refs.pop(0) if has_own else None
    residual, weight, kept_in, outgoing, kept, chosen = refs
    del kept_in
    is_base, depth = place[0], place[1]
    chunk = step - 1 - depth
    inputs = entry_rows(depth, 0, own, arrived, chosen)
    width = weight.shape[1]
    size = min(tile, width)

    @pl.loop(0, width // size)
    def _(index):
        part = columns_of(index, size)
        product = jnp.dot(inputs[...], weight[:, part], preferred_element_type=jnp.float32)
        added = jnp.where(is_base == 1, residual[:, part], 0.0)
        total = inputs[:, part].astype(jnp.float32) + gelu_value(product) + added
        outgoing[:, part] = total.astype(jnp.bfloat16)

        @pl.when(in_chunks(chunk))
        def _():
            kept[jnp.clip(chunk, 0, chunk_count - 1), :, part] = product


def residual_kernel(
    step, place, received, outgoing, zero_rows, second_rows, sides_in, residual, sides
):
    del sides_in
    half, width = zero_rows.shape
    size = min(tile // 3, width)
    chunk = step - place[1]
    slot = jnp.clip(chunk, 0, chunk_count - 1)

    @pl.when(place[0] == 1)
    def _():
        @pl.loop(0, width // size)
        def _(index):
            part = columns_of(index, size)
            residual[:, part] = jnp.dot(
                received[:, :half], zero_rows[:, part], preferred_element_type=jnp.float32
            ) + jnp.dot(
                received[:, half:], second_rows[:, part], preferred_element_type=jnp.float32
            )

    @pl.when((place[0] == 0) & in_chunks(chunk))
    def _():
        sides[slot] = outgoing[...]


def back_kernel(step, last_depth, has_arrived, has_own, *refs):
    refs = list(refs)
    place = refs.pop(0)
    arrived = refs.pop(0) if has_arrived else None
    own = refs.pop(0) if has_own else None
    slopes, weight, kept_in, outgoing, kept, chosen, scaled = refs
    del kept_in
    chunk = step - (last_depth - place[1])
    slot = jnp.clip(chunk, 0, chunk_count - 1)
    grad = entry_rows(place[1], last_depth, own, arrived, chosen)
    width = weight.shape[1]
    size = min(tile, width)
    scaled[...] = (grad[...].astype(jnp.float32) * slopes[slot]).astype(jnp.bfloat16)

    @pl.loop(0, width // size)
    def _(index):
        part = columns_of(index, size)
        back_term = lax.dot_general(
            scaled[...],
            weight[part, :],
            (((1,), (1,)), ((), ())),
            preferred_element_type=jnp.float32,
        )
        outgoing[:, part] = (grad[:, part].astype(jnp.float32) + back_term).astype(jnp.bfloat16)

    @pl.when(in_chunks(chunk))
    def _():
        kept[slot] = grad[...]


def spread_kernel(place, sides, picks, *parts):
    half = picks.shape[1]

    @pl.when(place[0] == 0)
    def _():
        for shift, part in enumerate(parts):
            for chunk in range(chunk_count):
                for second in range(2):
                    part[chunk, second] = jnp.dot(
                        sides[chunk, :, second * half : (second + 1) * half],
                        picks[shift],
                        preferred_element_type=jnp.float32,
                    ).astype(jnp.bfloat16)


def finish_kernel(place, arrived, shared, kept, grads):
    @pl.when(place[1] == 0)
    def _():
        for chunk in range(chunk_count - 1):
            grads[chunk] = kept[chunk]
        grads[chunk_count - 1] = arrived[...]

    @pl.when(place[1] != 0)
    def _():
        grads[...] = shared[...]


def reduce_kernel(place, *refs):
    parts, grads, (second_value, first_value) = refs[:x_size], refs[x_size : 2 * x_size], refs[-2:]
    width = first_value.shape[1]
    size = min(512, width)

    @pl.when(place[0] == 0)
    def _():
        @pl.loop(0, width // size)
        def _(index):
            columns = columns_of(index, size)
            for second, target in enumerate((first_value, second_value)):
                total = None
                for part, grad in zip(parts, grads):
                    for chunk in range(chunk_count):
                        term = lax.dot_general(
                            part[chunk, second],
                            grad[chunk, :, columns],
                            (((0,), (0,)), ((), ())),
                            preferred_element_type=jnp.float32,
                        )
                        total = term if total is None else total + term
                target[:, columns] = total.astype(target.dtype)


def slope_kernel(products, slopes):
    width = products.shape[-1]
    size = min(256, width)

    @pl.loop(0, width // size)
    def _(index):
        part = columns_of(index, size)
        for chunk in range(chunk_count):
            slopes[chunk, :, part] = gelu_slope(products[chunk, :, part])


def body(latents, control_hint, upstream, batch_order, section_weight, zero_weight):
    section_count = lax.axis_size("section")
    dp_count = lax.axis_size("dp")
    z_size = dp_count // x_size
    block_count = section_count // 2
    section_place = lax.axis_index("section")
    dp_place = lax.axis_index("dp")
    x_place = dp_place % x_size
    z_place = dp_place // x_size
    depth = section_place // 2
    is_base = section_place % 2 == 0
    weight = section_weight[0]
    zero_rows = zero_weight[0]
    width = weight.shape[0]
    half = zero_rows.shape[0]
    all_rows = latents.shape[0] * latents.shape[1]
    rows = all_rows // chunk_count

    def mirrored(place):
        return (z_size - 1 - place // x_size) * x_size + place % x_size

    def move(value, section_pairs, flip):
        pairs = [
            (source * dp_count + place, target * dp_count + (mirrored(place) if flip else place))
            for source, target in section_pairs
            for place in range(dp_count)
        ]
        return lax.ppermute(value, both_axes, pairs)

    def active_blocks(step):
        return [
            step - chunk for chunk in range(chunk_count) if 0 <= step - chunk < block_count
        ]

    to_base = [(2 * block + 1, 2 * block) for block in range(block_count)]
    to_control = [(2 * block, 2 * block + 1) for block in range(block_count)]

    shared_span = max(block_count // 2, chunk_count + 2)

    def forward_hops(step):
        steps = range(step % shared_span, block_count + chunk_count - 1, shared_span)
        return sorted(
            {
                (2 * block + 1 - lag, 2 * block + 3 - lag)
                for each in steps
                for lag in (0, 1)
                for block in active_blocks(each - lag)
                if block + 1 < block_count
            }
        )

    def backward_hops(step):
        steps = range(step % shared_span, block_count + chunk_count - 2, shared_span)
        return sorted(
            {
                (
                    2 * (block_count - 1 - back),
                    max(1, 2 * (block_count - 2 - back)),
                )
                for each in steps
                for back in active_blocks(each)
                if back + 1 < block_count
            }
        )

    second_rows = move(zero_rows, to_base, False)
    ordered = jnp.take(latents, batch_order, axis=0)
    hinted = jnp.take(control_hint, batch_order, axis=0)
    started = (ordered.astype(jnp.float32) + hinted.astype(jnp.float32)).astype(jnp.bfloat16)
    first_rows = jnp.where(is_base, ordered, started).reshape(chunk_count, rows, width)
    own_upstream = upstream.reshape(chunk_count, rows, width)
    first_rows = [first_rows[chunk] for chunk in range(chunk_count)]
    own_upstream = [own_upstream[chunk] for chunk in range(chunk_count)]
    quarter = half // x_size
    pick_shape = (x_size, half, quarter)
    piece = quarter // z_size
    within = lax.broadcasted_iota(jnp.int32, pick_shape, 2)
    order = within // piece
    z_target = jnp.zeros_like(order)
    distance = 1
    while distance < z_size:
        z_target = z_target + (order // (z_size // (2 * distance))) % 2 * distance
        distance *= 2
    x_target = (x_place - lax.broadcasted_iota(jnp.int32, pick_shape, 0)) % x_size
    wanted = (z_target * x_size + x_target) * piece + within % piece
    picks = (lax.broadcasted_iota(jnp.int32, pick_shape, 1) == wanted).astype(jnp.bfloat16)
    first_rows, own_upstream, picks = lax.optimization_barrier((first_rows, own_upstream, picks))
    upstream_rows = [move(part, forward_hops(block_count), True) for part in own_upstream]

    place = jnp.stack([is_base.astype(jnp.int32), depth])
    row_buffer = pltpu.VMEM((rows, width), jnp.bfloat16)
    row_shape = jax.ShapeDtypeStruct((rows, width), jnp.bfloat16)
    arrived = None
    residual = jnp.zeros((rows, width), jnp.float32)
    products = jnp.zeros((chunk_count, rows, width), jnp.float32)
    sides = jnp.zeros((chunk_count, rows, width), jnp.bfloat16)
    for step in range(block_count + chunk_count):
        entering = ()
        if step == 4:
            upstream_rows, arrived = lax.optimization_barrier((upstream_rows, arrived))
        if arrived is not None:
            entering += (arrived,)
        if step <= chunk_count:
            entering += (
                jnp.where(
                    is_base, first_rows[max(step - 1, 0)], first_rows[min(step, chunk_count - 1)]
                ),
            )
        outgoing, products = local_call(
            functools.partial(layer_kernel, step, arrived is not None, step <= chunk_count),
            (place,) + entering + (residual, weight, products),
            (row_shape, shape_of(products)),
            2 * rows * width * width,
            {3 + len(entering): 1},
            (row_buffer,),
        )
        if step < block_count + chunk_count - 1:
            arrived = move(outgoing, forward_hops(step), True)
        if step < block_count + chunk_count - 1:
            received = move(outgoing, to_base, False)
            residual, sides = local_call(
                functools.partial(residual_kernel, step),
                (place, received, outgoing, zero_rows, second_rows, sides),
                (shape_of(residual), shape_of(sides)),
                256,
                {5: 1},
            )

    (slopes,) = local_call(
        lambda unused, products_in, slopes_out: slope_kernel(products_in, slopes_out),
        (place, products),
        (shape_of(products),),
        256,
        {},
    )

    def along_x(value, shift):
        pairs = [
            (section * dp_count + z * x_size + (x + shift) % x_size, section * dp_count + z * x_size + x)
            for section in range(1, section_count, 2)
            for z in range(z_size)
            for x in range(x_size)
        ]
        return lax.ppermute(value, both_axes, pairs)

    def spread_side(side):
        part_shape = jax.ShapeDtypeStruct((chunk_count, 2, rows, quarter), jnp.bfloat16)
        parts = local_call(spread_kernel, (place, side, picks), (part_shape,) * x_size, 256, {})
        return [parts[0]] + [along_x(parts[shift], shift) for shift in range(1, x_size)]

    grads = jnp.zeros((chunk_count, rows, width), jnp.bfloat16)
    spread = joined = None
    for step in range(block_count + chunk_count - 1):
        if step == block_count // 2:
            joined = sides
        if step == block_count // 2 + 1:
            spread, arrived = lax.optimization_barrier((spread, arrived))
        entering = ()
        if step > 0:
            entering += (arrived,)
        if step < chunk_count:
            entering += (upstream_rows[step],)
        if step < block_count + chunk_count - 2:
            outgoing, grads = local_call(
                functools.partial(
                    back_kernel, step, block_count - 1, step > 0, step < chunk_count
                ),
                (place,) + entering + (slopes, weight, grads),
                (row_shape, shape_of(grads)),
                2 * rows * width * width,
                {3 + len(entering): 1},
                (row_buffer, row_buffer),
            )
            arrived = move(outgoing, backward_hops(step), True)
            if step == block_count // 2:
                joined, outgoing = lax.optimization_barrier((joined, outgoing))
                spread = spread_side(joined)

    (grads,) = local_call(
        finish_kernel,
        (place, arrived, move(grads, to_control, False), grads),
        (shape_of(grads),),
        256,
        {},
    )
    value_shape = (quarter, width)
    control_value, base_value = local_call(
        reduce_kernel,
        (place, *spread, grads) + tuple(along_x(grads, shift) for shift in range(1, x_size)),
        (
            jax.ShapeDtypeStruct(value_shape, jnp.float32),
            jax.ShapeDtypeStruct(value_shape, jnp.bfloat16),
        ),
        256,
        {},
    )
    base_value = move(base_value, to_base, False)
    partial_value = jnp.where(is_base, base_value.astype(jnp.float32), control_value).reshape(
        z_size, half // dp_count, width
    )
    distance = 1
    while distance < z_size:
        upper = (z_place // distance) % 2
        kept_size = partial_value.shape[0] // 2
        kept = lax.dynamic_slice_in_dim(partial_value, upper * kept_size, kept_size, 0)
        sent = lax.dynamic_slice_in_dim(partial_value, (1 - upper) * kept_size, kept_size, 0)
        pairs = [
            (place, ((place // x_size) ^ distance) * x_size + place % x_size)
            for place in range(dp_count)
        ]
        partial_value = kept + lax.ppermute(sent.astype(jnp.bfloat16), "dp", pairs).astype(
            jnp.float32
        )
        distance *= 2
    grad_scale = 1.0 / math.sqrt(all_rows * dp_count)
    return partial_value * grad_scale


def solution(mesh):
    placed = (
        P(None, "dp", None),
        P(None, "dp", None),
        P(None, "dp", None),
        P(),
        P("section", None, None),
        P("section", None, None),
    )
    return jax.shard_map(
        body, mesh=mesh, in_specs=placed, out_specs=P("section", "dp", None), check_vma=False
    )
```
